32 devices in a mesh: dp: 8 (over y, x, core), mp: 4 (over z).
Axes of the slice: x: 2, y: 2, z: 4, core: 2. Of those that a mesh axis runs over, the one named last changes fastest.
Arguments:
- tokens: bfloat16 [8192, 2048], P(('dp', 'mp')), may hold values from -6 to 6
- valid: int32 [8], P('dp'), may hold values from 256 to 1024, as said below
- attn_gain: float32 [2048], replicated, may hold values from 0.25 to 1.75
- w_query: bfloat16 [2048, 2048], replicated, may hold values from -0.125 to 0.125
- w_key: bfloat16 [2048, 2048], replicated, may hold values from -0.125 to 0.125
- w_value: bfloat16 [2048, 2048], replicated, may hold values from -0.125 to 0.125
- w_rank: bfloat16 [2048, 16], replicated, may hold values from -0.125 to 0.125
- w_forget: bfloat16 [16, 256], replicated, may hold values from -1.5 to 1.5
- forget_bias: float32 [256], replicated, may hold values from -2 to 6
- head_gain: float32 [512], replicated, may hold values from 0.25 to 1.75
- w_out: bfloat16 [2048, 2048], replicated, may hold values from -0.125 to 0.125
- mlp_gain: float32 [2048], replicated, may hold values from 0.25 to 1.75
- w_gate: bfloat16 [2048, 5632], P(None, 'mp'), may hold values from -0.125 to 0.125
- w_up: bfloat16 [2048, 5632], P(None, 'mp'), may hold values from -0.125 to 0.125
- w_down: bfloat16 [5632, 2048], P('mp'), may hold values from -0.15625 to 0.15625
- cotangent: bfloat16 [8192, 2048], P(('dp', 'mp')), may hold values from -6 to 6
Outputs:
- output: bfloat16 [8192, 2048], P(('dp', 'mp'))
- grad_tokens: float32 [8192, 2048], P(('dp', 'mp'))
- grad_attn_gain: float32 [2048], P('dp')
- grad_query: float32 [2048, 2048], P('dp', 'mp')
- grad_key: float32 [2048, 2048], P('dp', 'mp')
- grad_value: float32 [2048, 2048], P('dp', 'mp')
- grad_rank: float32 [2048, 16], P('dp')
- grad_forget: float32 [16, 256], P(None, 'dp')
- grad_forget_bias: float32 [256], P('dp')
- grad_head_gain: float32 [512], P('dp')
- grad_out: float32 [2048, 2048], P('dp', 'mp')
- grad_mlp_gain: float32 [2048], P('dp')
- grad_gate: float32 [2048, 5632], P('dp', 'mp')
- grad_up: float32 [2048, 5632], P('dp', 'mp')
- grad_down: float32 [5632, 2048], P('mp', 'dp')
The draws below stay inside these ranges and needn't reach their ends.
Inputs may be any that keep to these rules, and one draw needn't show every extreme that they name: Each bucket holds one sequence whose first valid tokens count; one bucket is full in every draw.
All inputs are finite; a program needn't handle non-finite values.
Results may differ from the reference program's by a relative error of at most 0.018.
Values may be sent and summed in bfloat16 or wider, within the bound.
No kernel may reach another device: no remote copies, remote signals or barrier semaphores. Data moves between devices by JAX's collectives and lax.ppermute only.
A program may use at most 448 MiB of HBM per device.

```python
import math
import jax
import jax.numpy as jnp
from jax import lax

D = 2048
HEADS = 4
HEAD_DIMENSION = 512
SLOTS = 64
RANK = 16
FF = 5632
LEN = 1024
BLOCK = 128
GROUPS = 8
TOKENS = 8192


def draw_valid(key, part):
    first_key, second_key = jax.random.split(jax.random.fold_in(key, 11))
    counts = jax.random.randint(first_key, (GROUPS,), LEN // 4, LEN + 1)
    chosen = jax.random.randint(second_key, (), 0, GROUPS)
    return jnp.where(jnp.arange(GROUPS) == chosen, LEN, counts).astype(jnp.int32)


def block_scale(stream_key, shape, cuts, low, top_value):
    def one(dim, parts):
        steps = jax.random.uniform(jax.random.fold_in(jax.random.fold_in(stream_key, 6), dim), (parts,), jnp.float32, low / len(cuts), top_value / len(cuts))
        return jnp.repeat(jnp.exp(steps), shape[dim] // parts).reshape((-1,) + (1,) * (len(shape) - dim - 1))

    level = one(*cuts[0])
    for cut in cuts[1:]:
        level = level * one(*cut)
    return level


def normal_values(own_key, shape, deviation, bound, cuts=(), dtype=jnp.bfloat16):
    values = deviation * jax.random.normal(own_key, shape, jnp.float32)
    if cuts:
        values = values * block_scale(own_key, shape, cuts, -0.22, 0.18)
    return jnp.clip(values, -bound, bound).astype(dtype)


def setup_inputs(seed: int = 0) -> dict:
    keys = jax.random.split(jax.random.key(seed), 17)
    tokens = normal_values(keys[0], (TOKENS, D), 1.0, 6.0, ((0, 32),))
    valid = draw_valid(jax.random.fold_in(keys[16], 71), 0)
    attn_gain = jnp.clip(1.0 + 0.15 * jax.random.normal(keys[2], (D,), jnp.float32), 0.25, 1.75)
    w_query = normal_values(keys[3], (D, D), D ** -0.5, 0.125)
    w_key = normal_values(keys[4], (D, D), D ** -0.5, 0.125)
    w_value = normal_values(keys[5], (D, D), D ** -0.5, 0.125)
    w_rank = normal_values(keys[6], (D, RANK), D ** -0.5, 0.125)
    w_forget = normal_values(keys[7], (RANK, HEADS * SLOTS), RANK ** -0.5, 1.5)
    forget_bias = jnp.clip(jax.random.uniform(keys[8], (HEADS * SLOTS,), jnp.float32, -2.0, 6.0), -2.0, 6.0)
    head_gain = jnp.clip(1.0 + 0.15 * jax.random.normal(keys[9], (HEAD_DIMENSION,), jnp.float32), 0.25, 1.75)
    w_out = normal_values(keys[10], (D, D), D ** -0.5, 0.125)
    mlp_gain = jnp.clip(1.0 + 0.15 * jax.random.normal(keys[11], (D,), jnp.float32), 0.25, 1.75)
    w_gate = normal_values(keys[12], (D, FF), D ** -0.5, 0.125, ((1, 4),))
    w_up = normal_values(keys[13], (D, FF), D ** -0.5, 0.125, ((1, 4),))
    w_down = normal_values(keys[14], (FF, D), (FF // 4) ** -0.5, 0.15625, ((0, 4),))
    cotangent = normal_values(keys[15], (TOKENS, D), 1.0, 6.0, ((0, 32),))
    return dict(tokens=tokens, valid=valid, attn_gain=attn_gain, w_query=w_query, w_key=w_key, w_value=w_value, w_rank=w_rank, w_forget=w_forget, forget_bias=forget_bias, head_gain=head_gain, w_out=w_out, mlp_gain=mlp_gain, w_gate=w_gate, w_up=w_up, w_down=w_down, cotangent=cotangent)


EPS = 1e-06
GATE_NORM = 8.0
HIGH_PRECISION = lax.Precision.HIGHEST

@jax.custom_vjp
def low(v):
    return lax.optimization_barrier(v.astype(jnp.bfloat16)).astype(jnp.float32)

@jax.custom_vjp
def low_back(v):
    return v

def low_keep(v):
    return (low(v), None)

def low_pass(kept, grad):
    return (grad,)

def back_keep(v):
    return (v, None)

def back_low(kept, grad):
    return (low(grad),)
low.defvjp(low_keep, low_pass)
low_back.defvjp(back_keep, back_low)

def mult(left, right):
    return jnp.dot(left, right, precision=HIGH_PRECISION, preferred_element_type=jnp.float32)

def rms_norm(values, gain):
    return values * lax.rsqrt(lax.optimization_barrier(jnp.mean(values * values, axis=-1, keepdims=True)) + EPS) * gain

def token_step(states, inputs):
    key_slot_state, value_slot_state = states
    query_rows, key_row_block, value_row_block, decay = inputs
    keep = decay[:, :, None]
    fresh = (1.0 - decay)[:, :, None]
    key_slot_state = keep * key_slot_state + fresh * key_row_block[:, None, :]
    value_slot_state = keep * value_slot_state + fresh * value_row_block[:, None, :]
    attention_scores = jnp.einsum('ces,cs->ce', key_slot_state, query_rows, precision=HIGH_PRECISION) / math.sqrt(HEAD_DIMENSION)
    attention_probabilities = jax.nn.softmax(attention_scores, axis=-1)
    output_rows = jnp.einsum('qs,qsn->qn', attention_probabilities, value_slot_state, precision=HIGH_PRECISION)
    return ((key_slot_state, value_slot_state), output_rows)

def slot_block(states, block):
    return lax.scan(token_step, states, block)

def group_mix(inputs):
    steps = LEN // BLOCK
    blocks = tuple((member.reshape((steps, BLOCK) + member.shape[1:]) for member in inputs))
    blank_state = jnp.zeros((HEADS, SLOTS, HEAD_DIMENSION), jnp.float32)
    _, output_rows = lax.scan(jax.checkpoint(slot_block), (blank_state, blank_state), blocks)
    return output_rows.reshape(inputs[0].shape)

def reference(tokens, valid, attn_gain, w_query, w_key, w_value, w_rank, w_forget, forget_bias, head_gain, w_out, mlp_gain, w_gate, w_up, w_down, cotangent):
    valid_mask = (jnp.arange(LEN)[None, :] < valid[:, None]).astype(jnp.float32).reshape(TOKENS, 1)

    def forward(resid, gain_one, query_w, key_w, value_w, rank_w, forget_w, bias, gain_head, out_w, gain_two, gate_w, up_w, down_w):
        normed = low(rms_norm(resid, gain_one))
        query_rows = low(jax.nn.silu(low_back(mult(normed, query_w))))
        key_row_block = low(jax.nn.silu(low_back(mult(normed, key_w))))
        value_row_block = low(low_back(mult(normed, value_w)))
        rank_rows = low_back(mult(normed, rank_w))
        decay = jnp.exp(jax.nn.log_sigmoid(mult(rank_rows, forget_w) + bias) / GATE_NORM)
        shaped = (query_rows.reshape(GROUPS, LEN, HEADS, HEAD_DIMENSION), key_row_block.reshape(GROUPS, LEN, HEADS, HEAD_DIMENSION), value_row_block.reshape(GROUPS, LEN, HEADS, HEAD_DIMENSION), decay.reshape(GROUPS, LEN, HEADS, SLOTS))
        mixed = lax.map(group_mix, shaped).reshape(TOKENS, HEADS, HEAD_DIMENSION)
        attn_low = low(rms_norm(mixed, gain_head).reshape(TOKENS, D))
        hidden_res = resid + low_back(mult(attn_low, out_w))
        mlp_low = low(rms_norm(hidden_res, gain_two))
        gate_pre = low_back(mult(mlp_low, gate_w))
        up_pre = low_back(mult(mlp_low, up_w))
        inner = low(jax.nn.silu(gate_pre) * up_pre)
        return (hidden_res + mult(inner, down_w)) * valid_mask
    floats = tuple((member.astype(jnp.float32) for member in (tokens, attn_gain, w_query, w_key, w_value, w_rank, w_forget, forget_bias, head_gain, w_out, mlp_gain, w_gate, w_up, w_down)))
    result, pull = jax.vjp(forward, *floats)
    grads = pull(cotangent.astype(jnp.float32))
    return (result.astype(jnp.bfloat16), grads[0], grads[1], grads[2], grads[3], grads[4], grads[5], grads[6], grads[7], grads[8], grads[9], grads[10], grads[11], grads[12], grads[13])
```

```python
import functools
import math

import jax
import jax.numpy as jnp
from jax import lax
from jax.experimental import pallas as pl
from jax.experimental.pallas import tpu as pltpu
from jax.sharding import PartitionSpec as P

HEADS = 4
CHUNK = 128
LANES = 128
EPS = 1e-06
GATE_NORM = 8.0
RANGE_LIMIT = 60.0
HIGH_PRECISION = lax.Precision.HIGHEST
NN = (((1,), (0,)), ((), ()))
TN = (((0,), (0,)), ((), ()))
NT = (((1,), (1,)), ((), ()))


def low(values):
    return values.astype(jnp.bfloat16)


def product(left, right, dims=NN):
    return lax.dot_general(left, right, dims, preferred_element_type=jnp.float32)


def fine(left, right, dims=NN):
    return lax.dot_general(
        left, right, dims, precision=HIGH_PRECISION, preferred_element_type=jnp.float32
    )


def silu_slope(raw):
    sigmoid = jax.nn.sigmoid(raw)
    return sigmoid * (1.0 + raw * (1.0 - sigmoid))


def sigmoid(raw):
    return 1.0 / (1.0 + jnp.exp(-raw))


def iota(shape, axis):
    return lax.broadcasted_iota(jnp.int32, shape, axis)


def column_of(row):
    size = row.shape[1]
    eye = iota((size, size), 0) == iota((size, size), 1)
    return jnp.sum(jnp.where(eye, row, 0.0), axis=1, keepdims=True)


def row_of(column):
    size = column.shape[0]
    eye = iota((size, size), 0) == iota((size, size), 1)
    return jnp.sum(jnp.where(eye, column, 0.0), axis=0, keepdims=True)


def causal_mask(size):
    return iota((size, size), 0) >= iota((size, size), 1)


def decays(rank, forget, bias):
    logits = fine(rank, forget) + bias
    log_decay = (jnp.minimum(logits, 0.0) - jnp.log1p(jnp.exp(-jnp.abs(logits)))) / GATE_NORM
    size = rank.shape[0]
    total = fine(causal_mask(size).astype(jnp.float32), log_decay)
    return logits, log_decay, total


def direct_factors(total):
    size = total.shape[0]
    middle = 0.5 * total[size - 1 :, :]
    return causal_mask(size), jnp.exp(total - middle), jnp.exp(middle - total)


def level_factors(total, level):
    size = total.shape[0]
    half = jnp.left_shift(1, level)
    row, column = iota((size, size), 0), iota((size, size), 1)
    row_span = jnp.right_shift(row, level + 1)
    mask = (
        (row_span == jnp.right_shift(column, level + 1))
        & (jnp.bitwise_and(row, half) != 0)
        & (jnp.bitwise_and(column, half) == 0)
    )
    pick = column == jnp.left_shift(row_span, level + 1) + half - 1
    middle = fine(pick.astype(jnp.float32), total)
    return (
        mask,
        jnp.exp(jnp.minimum(total - middle, 0.0)),
        jnp.exp(jnp.minimum(middle - total, 0.0)),
    )


def over_levels(total, first, term):
    size = total.shape[0]
    eye = iota((size, size), 0) == iota((size, size), 1)
    ones = jnp.ones_like(total)
    start = first((eye, ones, ones))
    count = size.bit_length() - 1

    def body(level, running):
        return jax.tree.map(jnp.add, running, term(level_factors(total, level)))

    return lax.fori_loop(0, count, body, start)


def forward_kernel(
    q_ref,
    k_ref,
    v_ref,
    rank_ref,
    forget_ref,
    bias_ref,
    gain_ref,
    a_ref,
    o_ref,
    soft_ref,
    kept_ref,
    key_state,
    value_state,
    score_ref,
    mix_ref,
):
    @pl.when(pl.program_id(0) == 0)
    def _():
        key_state[...] = jnp.zeros_like(key_state)
        value_state[...] = jnp.zeros_like(value_state)

    kept_ref[0, 0] = key_state[...]
    kept_ref[0, 1] = value_state[...]
    size = q_ref.shape[0]
    slots = bias_ref.shape[1]
    scale = 1.0 / math.sqrt(q_ref.shape[1])
    q_raw, k_raw = q_ref[...], k_ref[...]
    q, k, v = low(q_raw * sigmoid(q_raw)), low(k_raw * sigmoid(k_raw)), low(v_ref[...])
    _, log_decay, total = decays(rank_ref[...], forget_ref[...], bias_ref[...])
    fresh = 1.0 - jnp.exp(log_decay)
    last = total[size - 1 :, :]
    from_start = jnp.exp(total)
    direct = product(q, k, NT)
    carried = from_start * product(q, low(key_state[...]), NT)
    narrow = jnp.max(-last) <= RANGE_LIMIT

    def intra_scores(factors):
        mask, late, early = factors
        return late * fine(jnp.where(mask, direct, 0.0), early * fresh)

    def soft(scores):
        return jax.nn.softmax(scores, axis=-1)

    def intra_mix(weights):
        def term(factors):
            mask, late, early = factors
            return jnp.where(mask, fine(weights * late, early * fresh, NT), 0.0)

        return term

    @pl.when(narrow)
    def _():
        factors = direct_factors(total)
        scores = (intra_scores(factors) + carried) * scale
        score_ref[...] = scores
        mix_ref[...] = intra_mix(soft(scores))(factors)

    @pl.when(jnp.logical_not(narrow))
    def _():
        scores = (over_levels(total, intra_scores, intra_scores) + carried) * scale
        score_ref[...] = scores
        term = intra_mix(soft(scores))
        mix_ref[...] = over_levels(total, term, term)

    scores = score_ref[...]
    weights = soft(scores)
    soft_ref[:, :slots] = scores
    soft_ref[:, slots:] = weights
    out = product(low(weights * from_start), low(value_state[...])) + product(
        low(mix_ref[...]), v
    )
    o_ref[...] = out
    a_ref[...] = low(
        out * lax.rsqrt(jnp.mean(out * out, axis=-1, keepdims=True) + EPS) * gain_ref[...]
    )
    to_end = low(jnp.exp(last - total) * fresh)
    keep = column_of(jnp.exp(last))
    key_state[...] = keep * key_state[...] + product(to_end, k, TN)
    value_state[...] = keep * value_state[...] + product(to_end, v, TN)


def backward_kernel(
    q_ref,
    k_ref,
    v_ref,
    rank_ref,
    o_ref,
    soft_ref,
    kept_ref,
    da_ref,
    forget_ref,
    bias_ref,
    gain_ref,
    draw_ref,
    dforget_ref,
    dbias_ref,
    dgain_ref,
    key_back,
    value_back,
    dp_ref,
    da_part_ref,
    mix_ref,
    early_ref,
):
    @pl.when(pl.program_id(0) == 0)
    def _():
        key_back[...] = jnp.zeros_like(key_back)
        value_back[...] = jnp.zeros_like(value_back)
        dforget_ref[...] = jnp.zeros_like(dforget_ref)
        dbias_ref[...] = jnp.zeros_like(dbias_ref)
        dgain_ref[...] = jnp.zeros_like(dgain_ref)

    size, width = q_ref.shape
    slots = bias_ref.shape[1]
    scale = 1.0 / math.sqrt(width)
    q_raw, k_raw = q_ref[...], k_ref[...]
    q_sig, k_sig = sigmoid(q_raw), sigmoid(k_raw)
    q, k, v = low(q_raw * q_sig), low(k_raw * k_sig), low(v_ref[...])
    rank, forget = rank_ref[...], forget_ref[...]
    logits, log_decay, total = decays(rank, forget, bias_ref[...])
    decay = jnp.exp(log_decay)
    fresh = 1.0 - decay
    last = total[size - 1 :, :]
    from_start = jnp.exp(total)
    to_end = jnp.exp(last - total)
    narrow = jnp.max(-last) <= RANGE_LIMIT
    scores, weights = soft_ref[:, :slots], soft_ref[:, slots:]
    key_start, value_start = kept_ref[0, 0], kept_ref[0, 1]
    key_end, value_end = key_back[...], value_back[...]

    out, da = o_ref[...], da_ref[...].astype(jnp.float32)
    inverse = lax.rsqrt(jnp.mean(out * out, axis=-1, keepdims=True) + EPS)
    unit = out * inverse
    dgain_ref[...] += jnp.sum(da * unit, axis=0, keepdims=True)
    scaled = da * gain_ref[...]
    do = low(inverse * (scaled - unit * jnp.mean(scaled * unit, axis=-1, keepdims=True)))

    direct = product(q, k, NT)
    dmix = product(do, v, NT)
    dp_carried = from_start * product(do, low(value_start), NT)

    def intra_dp(factors):
        mask, late, early = factors
        return late * fine(jnp.where(mask, dmix, 0.0), early * fresh)

    def back_scores(dp):
        return weights * (dp - jnp.sum(weights * dp, axis=-1, keepdims=True))

    def intra_back(ds):
        def term(factors):
            mask, late, early = factors
            ds_late, p_late, factor = ds * late, weights * late, early * fresh
            return (
                jnp.where(mask, fine(ds_late, factor, NT), 0.0),
                jnp.where(mask, fine(p_late, factor, NT), 0.0),
                early
                * (
                    fine(jnp.where(mask, direct, 0.0), ds_late, TN)
                    + fine(jnp.where(mask, dmix, 0.0), p_late, TN)
                ),
            )

        return term

    def store(dp, parts):
        dp_ref[...] = dp
        da_part_ref[...], mix_ref[...], early_ref[...] = parts

    @pl.when(narrow)
    def _():
        factors = direct_factors(total)
        dp = intra_dp(factors) + dp_carried
        store(dp, intra_back(back_scores(dp) * scale)(factors))

    @pl.when(jnp.logical_not(narrow))
    def _():
        dp = over_levels(total, intra_dp, intra_dp) + dp_carried
        term = intra_back(back_scores(dp) * scale)
        store(dp, over_levels(total, term, term))

    dp = dp_ref[...]
    ds = back_scores(dp)
    ds_scaled = ds * scale
    ddirect, mix, early_sum = low(da_part_ref[...]), low(mix_ref[...]), early_ref[...]
    late_sum = ds * scores + weights * dp
    end_sum = to_end * (product(k, low(key_end), NT) + product(v, low(value_end), NT))
    carry = low(to_end * fresh)
    ds_start, p_start = low(ds_scaled * from_start), low(weights * from_start)

    dq = product(ddirect, k) + product(ds_start, low(key_start))
    dk = product(ddirect, q, TN) + product(carry, low(key_end))
    dv = product(mix, do, TN) + product(carry, low(value_end))
    draw_ref[:, :width] = low(dq * (q_sig * (1.0 + q_raw * (1.0 - q_sig))))
    draw_ref[:, width : 2 * width] = low(dk * (k_sig * (1.0 + k_raw * (1.0 - k_sig))))
    draw_ref[:, 2 * width : 3 * width] = low(dv)

    keep = jnp.exp(last)
    through = keep * row_of(
        jnp.sum(key_start * key_end + value_start * value_end, axis=1, keepdims=True)
    )
    after = (iota((size, size), 0) <= iota((size, size), 1)).astype(jnp.float32)
    before = (iota((size, size), 0) > iota((size, size), 1)).astype(jnp.float32)
    dlog = (
        fine(after, late_sum - fresh * early_sum)
        + fine(before, fresh * end_sum)
        + through
        - decay * (early_sum + end_sum)
    )
    dlogits = dlog * (1.0 / (1.0 + jnp.exp(logits))) / GATE_NORM
    dbias_ref[...] += jnp.sum(dlogits, axis=0, keepdims=True)
    dforget_ref[...] += fine(rank, dlogits, TN)
    draw_ref[:, 3 * width :] = low(fine(dlogits, forget, NT))

    keep_column = column_of(keep)
    key_back[...] = keep_column * key_end + product(ds_start, q, TN)
    value_back[...] = keep_column * value_end + product(p_start, do, TN)


def piece_specs(width, chunk, order):
    parts = [
        pl.BlockSpec((chunk, width), functools.partial(lambda part, i: (order(i), part), part))
        for part in range(3)
    ]
    rank = pl.BlockSpec((chunk, LANES), lambda i: (order(i), 3 * width // LANES))
    return parts + [rank]


def whole(shape):
    return pl.BlockSpec(shape, lambda i: (0,) * len(shape))


def mixer_forward(raw, forget, bias, gain):
    length, slots, width = raw.shape[0], bias.shape[1], gain.shape[1]
    steps = length // CHUNK

    def order(i):
        return i

    def rows(size):
        return pl.BlockSpec((CHUNK, size), lambda i: (order(i), 0))

    return pl.pallas_call(
        forward_kernel,
        grid=(steps,),
        in_specs=piece_specs(width, CHUNK, order)
        + [whole(forget.shape), whole(bias.shape), whole(gain.shape)],
        out_specs=(
            rows(width),
            rows(width),
            rows(2 * slots),
            pl.BlockSpec((1, 2, slots, width), lambda i: (i, 0, 0, 0)),
        ),
        out_shape=(
            jax.ShapeDtypeStruct((length, width), jnp.bfloat16),
            jax.ShapeDtypeStruct((length, width), jnp.float32),
            jax.ShapeDtypeStruct((length, 2 * slots), jnp.float32),
            jax.ShapeDtypeStruct((steps, 2, slots, width), jnp.float32),
        ),
        scratch_shapes=[
            pltpu.VMEM((slots, width), jnp.float32),
            pltpu.VMEM((slots, width), jnp.float32),
            pltpu.VMEM((CHUNK, slots), jnp.float32),
            pltpu.VMEM((CHUNK, CHUNK), jnp.float32),
        ],
        cost_estimate=pl.CostEstimate(
            flops=2 * length * width * 1024, bytes_accessed=length * width * 20, transcendentals=0
        ),
        name="mixer_forward",
    )(raw, raw, raw, raw, forget, bias, gain)


def mixer_backward(raw, out, soft, kept, da, forget, bias, gain):
    length, slots, width = raw.shape[0], bias.shape[1], gain.shape[1]
    steps = length // CHUNK

    def order(i):
        return steps - 1 - i

    def rows(size):
        return pl.BlockSpec((CHUNK, size), lambda i: (order(i), 0))

    return pl.pallas_call(
        backward_kernel,
        grid=(steps,),
        in_specs=piece_specs(width, CHUNK, order)
        + [
            rows(width),
            rows(2 * slots),
            pl.BlockSpec((1, 2, slots, width), lambda i: (order(i), 0, 0, 0)),
            rows(width),
            whole(forget.shape),
            whole(bias.shape),
            whole(gain.shape),
        ],
        out_specs=(
            rows(3 * width + LANES),
            whole(forget.shape),
            whole(bias.shape),
            whole(gain.shape),
        ),
        out_shape=(
            jax.ShapeDtypeStruct((length, 3 * width + LANES), jnp.bfloat16),
            jax.ShapeDtypeStruct(forget.shape, jnp.float32),
            jax.ShapeDtypeStruct(bias.shape, jnp.float32),
            jax.ShapeDtypeStruct(gain.shape, jnp.float32),
        ),
        scratch_shapes=[
            pltpu.VMEM((slots, width), jnp.float32),
            pltpu.VMEM((slots, width), jnp.float32),
            pltpu.VMEM((CHUNK, slots), jnp.float32),
            pltpu.VMEM((CHUNK, CHUNK), jnp.float32),
            pltpu.VMEM((CHUNK, CHUNK), jnp.float32),
            pltpu.VMEM((CHUNK, slots), jnp.float32),
        ],
        cost_estimate=pl.CostEstimate(
            flops=4 * length * width * 1024, bytes_accessed=length * width * 24, transcendentals=0
        ),
        name="mixer_backward",
    )(raw, raw, raw, raw, out, soft, kept, da, forget, bias, gain)


def inverse_rms(values):
    return lax.rsqrt(jnp.mean(values * values, axis=-1, keepdims=True) + EPS)


def norm_back(values, inverse, gain, grad):
    unit = values * inverse
    scaled = gain * grad
    grad_values = inverse * (scaled - unit * jnp.mean(scaled * unit, axis=-1, keepdims=True))
    return grad_values, jnp.sum(grad * unit, axis=0)


def local(
    tokens,
    valid,
    attn_gain,
    w_query,
    w_key,
    w_value,
    w_rank,
    w_forget,
    forget_bias,
    head_gain,
    w_out,
    mlp_gain,
    w_gate,
    w_up,
    w_down,
    cotangent,
):
    width = w_query.shape[0]
    head_size = width // HEADS
    slots = forget_bias.shape[0] // HEADS
    ranks = w_rank.shape[1]
    rows = tokens.shape[0]
    shards, shard = lax.axis_size("mp"), lax.axis_index("mp")
    copies = shards // HEADS
    own_width = width // shards
    head, part = shard // copies, shard % copies
    begin = shard * rows

    def own_rows(values):
        return lax.dynamic_slice_in_dim(values, begin, rows, 0)

    def head_columns(values, size):
        return lax.dynamic_slice_in_dim(values, head * size, size, values.ndim - 1)

    def own_part(values):
        if copies == 1:
            return values
        pieces = [
            lax.dynamic_slice_in_dim(values, i * head_size + part * own_width, own_width, 1)
            for i in range(values.shape[1] // head_size)
        ]
        return jnp.concatenate(pieces, axis=1)

    counted = (part == 0).astype(jnp.float32)
    own_mask = ((begin + jnp.arange(rows)) < valid[0])[:, None]
    own_cotangent = jnp.where(own_mask, cotangent, jnp.zeros_like(cotangent))
    gathered = lax.all_gather(tokens, "mp", axis=0, tiled=True)
    grad_output = lax.all_gather(own_cotangent, "mp", axis=0, tiled=True)

    w_inputs = jnp.concatenate(
        [head_columns(w, head_size) for w in (w_query, w_key, w_value)]
        + [jnp.pad(w_rank, ((0, 0), (0, LANES - ranks)))],
        axis=1,
    )
    forget = jnp.pad(
        head_columns(w_forget.astype(jnp.float32), slots), ((0, LANES - ranks), (0, 0))
    )
    bias = head_columns(forget_bias, slots)[None]
    gain = head_gain[None]

    resid = gathered.astype(jnp.float32)
    normed = low(resid * inverse_rms(resid) * attn_gain)
    raw = product(normed, w_inputs)
    a_head, mixed, soft, kept = mixer_forward(raw, forget, bias, gain)
    a_all = lax.all_gather(own_part(a_head), "mp", axis=1, tiled=True)
    hidden = resid + product(a_all, w_out)
    mlp_normed = low(hidden * inverse_rms(hidden) * mlp_gain)
    gate = product(mlp_normed, w_gate)
    up = product(mlp_normed, w_up)
    activated = jax.nn.silu(gate)
    inner = low(activated * up)
    grad_inner = product(grad_output, w_down, NT)
    grad_gate_low = low(grad_inner * up * silu_slope(gate))
    grad_up_low = low(grad_inner * activated)
    partial = product(grad_gate_low, w_gate, NT) + product(grad_up_low, w_up, NT)
    grad_normed = lax.psum_scatter(
        low(partial), "mp", scatter_dimension=0, tiled=True
    ).astype(jnp.float32)

    own_hidden = own_rows(hidden)
    grad_hidden, part_mlp_gain = norm_back(
        own_hidden, inverse_rms(own_hidden), mlp_gain, grad_normed
    )
    grad_hidden = grad_hidden + own_cotangent.astype(jnp.float32)
    grad_hidden_all = lax.all_gather(low(grad_hidden), "mp", axis=0, tiled=True)
    w_out_rows = lax.dynamic_slice_in_dim(w_out, head * head_size, head_size, 0)
    grad_a = product(grad_hidden_all, w_out_rows, NT)
    draw, part_forget, part_bias, part_head_gain = mixer_backward(
        raw, mixed, soft, kept, grad_a, forget, bias, gain
    )
    draw_inputs = own_part(draw[:, : 3 * head_size])
    draw_rank = draw[:, 3 * head_size :]
    if copies > 1:
        draw_rank = low(draw_rank.astype(jnp.float32) * counted)
        w_own = jnp.concatenate([own_part(w_inputs[:, : 3 * head_size]), w_inputs[:, 3 * head_size :]], axis=1)
        draw = jnp.concatenate([draw_inputs, draw_rank], axis=1)
    else:
        w_own = w_inputs
    partial_input = product(draw, w_own, NT)
    grad_input = lax.psum_scatter(
        low(partial_input), "mp", scatter_dimension=0, tiled=True
    ).astype(jnp.float32)
    own_resid = tokens.astype(jnp.float32)
    grad_resid, part_attn_gain = norm_back(
        own_resid, inverse_rms(own_resid), attn_gain, grad_input
    )
    grad_tokens = grad_hidden + grad_resid

    mlp_own = lax.psum_scatter(
        low(product(inner, w_down)), "mp", scatter_dimension=0, tiled=True
    ).astype(jnp.float32)
    output = low(jnp.where(own_mask, own_hidden + mlp_own, 0.0))

    def dp_sum(values, axis):
        return lax.psum_scatter(
            low(values), "dp", scatter_dimension=axis, tiled=True
        ).astype(jnp.float32)

    sum_down = dp_sum(product(inner, grad_output, TN), 1)
    sum_gate = dp_sum(product(mlp_normed, grad_gate_low, TN), 0)
    sum_up = dp_sum(product(mlp_normed, grad_up_low, TN), 0)
    own_grad_hidden = lax.dynamic_slice_in_dim(
        grad_hidden_all, shard * own_width, own_width, 1
    )
    sum_wout = dp_sum(product(a_all, own_grad_hidden, TN), 0)
    sum_inputs = dp_sum(product(normed, draw_inputs, TN), 0)
    sum_query, sum_key, sum_value = (
        sum_inputs[:, i * own_width : (i + 1) * own_width] for i in range(3)
    )
    part_rank = product(draw_rank[:, :ranks], normed, TN)

    def place(values):
        spread = jnp.zeros((values.shape[0], HEADS * slots), jnp.float32)
        return lax.dynamic_update_slice_in_dim(spread, values * counted, head * slots, 1)

    small = lax.psum(
        (
            part_rank,
            place(part_forget[:ranks]),
            place(part_bias),
            part_head_gain * counted,
            part_attn_gain[None],
            part_mlp_gain[None],
        ),
        ("dp", "mp"),
    )
    replicas, replica = lax.axis_size("dp"), lax.axis_index("dp")

    def own_slice(values):
        size = values.shape[1] // replicas
        return lax.dynamic_slice_in_dim(values, replica * size, size, 1)

    sum_rank, sum_forget, sum_bias, sum_head_gain, sum_attn_gain, sum_mlp_gain = (
        own_slice(values) for values in small
    )
    return (
        output,
        grad_tokens,
        sum_attn_gain[0],
        sum_query,
        sum_key,
        sum_value,
        sum_rank.T,
        sum_forget,
        sum_bias[0],
        sum_head_gain[0],
        sum_wout,
        sum_mlp_gain[0],
        sum_gate,
        sum_up,
        sum_down,
    )


def solution(mesh):
    return jax.shard_map(
        local,
        mesh=mesh,
        in_specs=(
            P(("dp", "mp"), None),
            P("dp"),
            P(),
            P(),
            P(),
            P(),
            P(),
            P(),
            P(),
            P(),
            P(),
            P(),
            P(None, "mp"),
            P(None, "mp"),
            P("mp", None),
            P(("dp", "mp"), None),
        ),
        out_specs=(
            P(("dp", "mp"), None),
            P(("dp", "mp"), None),
            P("dp"),
            P("dp", "mp"),
            P("dp", "mp"),
            P("dp", "mp"),
            P("dp", None),
            P(None, "dp"),
            P("dp"),
            P("dp"),
            P("dp", "mp"),
            P("dp"),
            P("dp", "mp"),
            P("dp", "mp"),
            P("mp", "dp"),
        ),
        check_vma=False,
    )
```

```python
import functools
import math

import jax
import jax.numpy as jnp
from jax import lax
from jax.experimental import pallas as pl
from jax.experimental.pallas import tpu as pltpu
from jax.sharding import PartitionSpec as P

HEADS = 4
CHUNK = 128
LANES = 128
EPS = 1e-06
GATE_NORM = 8.0
RANGE_LIMIT = 60.0
HIGH_PRECISION = lax.Precision.HIGHEST
NN = (((1,), (0,)), ((), ()))
TN = (((0,), (0,)), ((), ()))
NT = (((1,), (1,)), ((), ()))


def low(values):
    return values.astype(jnp.bfloat16)


def product(left, right, dims=NN):
    return lax.dot_general(left, right, dims, preferred_element_type=jnp.float32)


def fine(left, right, dims=NN):
    return lax.dot_general(
        left, right, dims, precision=HIGH_PRECISION, preferred_element_type=jnp.float32
    )


def silu_slope(raw):
    sigmoid = jax.nn.sigmoid(raw)
    return sigmoid * (1.0 + raw * (1.0 - sigmoid))


def sigmoid(raw):
    return 1.0 / (1.0 + jnp.exp(-raw))


def iota(shape, axis):
    return lax.broadcasted_iota(jnp.int32, shape, axis)


def column_of(row):
    size = row.shape[1]
    eye = iota((size, size), 0) == iota((size, size), 1)
    return jnp.sum(jnp.where(eye, row, 0.0), axis=1, keepdims=True)


def row_of(column):
    size = column.shape[0]
    eye = iota((size, size), 0) == iota((size, size), 1)
    return jnp.sum(jnp.where(eye, column, 0.0), axis=0, keepdims=True)


def causal_mask(size):
    return iota((size, size), 0) >= iota((size, size), 1)


def decays(rank, forget, bias):
    logits = fine(rank, forget) + bias
    log_decay = (jnp.minimum(logits, 0.0) - jnp.log1p(jnp.exp(-jnp.abs(logits)))) / GATE_NORM
    size = rank.shape[0]
    total = fine(causal_mask(size).astype(jnp.float32), log_decay)
    return logits, log_decay, total


def direct_factors(total):
    size = total.shape[0]
    middle = 0.5 * total[size - 1 :, :]
    return causal_mask(size), jnp.exp(total - middle), jnp.exp(middle - total)


def level_factors(total, level):
    size = total.shape[0]
    half = jnp.left_shift(1, level)
    row, column = iota((size, size), 0), iota((size, size), 1)
    row_span = jnp.right_shift(row, level + 1)
    mask = (
        (row_span == jnp.right_shift(column, level + 1))
        & (jnp.bitwise_and(row, half) != 0)
        & (jnp.bitwise_and(column, half) == 0)
    )
    pick = column == jnp.left_shift(row_span, level + 1) + half - 1
    middle = fine(pick.astype(jnp.float32), total)
    return (
        mask,
        jnp.exp(jnp.minimum(total - middle, 0.0)),
        jnp.exp(jnp.minimum(middle - total, 0.0)),
    )


def over_levels(total, first, term):
    size = total.shape[0]
    eye = iota((size, size), 0) == iota((size, size), 1)
    ones = jnp.ones_like(total)
    start = first((eye, ones, ones))
    count = size.bit_length() - 1

    def body(level, running):
        return jax.tree.map(jnp.add, running, term(level_factors(total, level)))

    return lax.fori_loop(0, count, body, start)


def forward_kernel(
    q_ref,
    k_ref,
    v_ref,
    rank_ref,
    forget_ref,
    bias_ref,
    gain_ref,
    a_ref,
    o_ref,
    soft_ref,
    kept_ref,
    key_state,
    value_state,
    score_ref,
    mix_ref,
):
    @pl.when(pl.program_id(0) == 0)
    def _():
        key_state[...] = jnp.zeros_like(key_state)
        value_state[...] = jnp.zeros_like(value_state)

    kept_ref[0, 0] = key_state[...]
    kept_ref[0, 1] = value_state[...]
    size = q_ref.shape[0]
    slots = bias_ref.shape[1]
    scale = 1.0 / math.sqrt(q_ref.shape[1])
    q_raw, k_raw = q_ref[...], k_ref[...]
    q, k, v = low(q_raw * sigmoid(q_raw)), low(k_raw * sigmoid(k_raw)), low(v_ref[...])
    _, log_decay, total = decays(rank_ref[...], forget_ref[...], bias_ref[...])
    fresh = 1.0 - jnp.exp(log_decay)
    last = total[size - 1 :, :]
    from_start = jnp.exp(total)
    direct = product(q, k, NT)
    carried = from_start * product(q, low(key_state[...]), NT)
    narrow = jnp.max(-last) <= RANGE_LIMIT

    def intra_scores(factors):
        mask, late, early = factors
        return late * fine(jnp.where(mask, direct, 0.0), early * fresh)

    def soft(scores):
        return jax.nn.softmax(scores, axis=-1)

    def intra_mix(weights):
        def term(factors):
            mask, late, early = factors
            return jnp.where(mask, fine(weights * late, early * fresh, NT), 0.0)

        return term

    @pl.when(narrow)
    def _():
        factors = direct_factors(total)
        scores = (intra_scores(factors) + carried) * scale
        score_ref[...] = scores
        mix_ref[...] = intra_mix(soft(scores))(factors)

    @pl.when(jnp.logical_not(narrow))
    def _():
        scores = (over_levels(total, intra_scores, intra_scores) + carried) * scale
        score_ref[...] = scores
        term = intra_mix(soft(scores))
        mix_ref[...] = over_levels(total, term, term)

    scores = score_ref[...]
    weights = soft(scores)
    soft_ref[:, :slots] = scores
    soft_ref[:, slots:] = weights
    out = product(low(weights * from_start), low(value_state[...])) + product(
        low(mix_ref[...]), v
    )
    o_ref[...] = out
    a_ref[...] = low(
        out * lax.rsqrt(jnp.mean(out * out, axis=-1, keepdims=True) + EPS) * gain_ref[...]
    )
    to_end = low(jnp.exp(last - total) * fresh)
    keep = column_of(jnp.exp(last))
    key_state[...] = keep * key_state[...] + product(to_end, k, TN)
    value_state[...] = keep * value_state[...] + product(to_end, v, TN)


def backward_kernel(
    q_ref,
    k_ref,
    v_ref,
    rank_ref,
    o_ref,
    soft_ref,
    kept_ref,
    da_ref,
    forget_ref,
    bias_ref,
    gain_ref,
    draw_ref,
    dforget_ref,
    dbias_ref,
    dgain_ref,
    key_back,
    value_back,
    dp_ref,
    da_part_ref,
    mix_ref,
    early_ref,
):
    @pl.when(pl.program_id(0) == 0)
    def _():
        key_back[...] = jnp.zeros_like(key_back)
        value_back[...] = jnp.zeros_like(value_back)
        dforget_ref[...] = jnp.zeros_like(dforget_ref)
        dbias_ref[...] = jnp.zeros_like(dbias_ref)
        dgain_ref[...] = jnp.zeros_like(dgain_ref)

    size, width = q_ref.shape
    slots = bias_ref.shape[1]
    scale = 1.0 / math.sqrt(width)
    q_raw, k_raw = q_ref[...], k_ref[...]
    q_sig, k_sig = sigmoid(q_raw), sigmoid(k_raw)
    q, k, v = low(q_raw * q_sig), low(k_raw * k_sig), low(v_ref[...])
    rank, forget = rank_ref[...], forget_ref[...]
    logits, log_decay, total = decays(rank, forget, bias_ref[...])
    decay = jnp.exp(log_decay)
    fresh = 1.0 - decay
    last = total[size - 1 :, :]
    from_start = jnp.exp(total)
    to_end = jnp.exp(last - total)
    narrow = jnp.max(-last) <= RANGE_LIMIT
    scores, weights = soft_ref[:, :slots], soft_ref[:, slots:]
    key_start, value_start = kept_ref[0, 0], kept_ref[0, 1]
    key_end, value_end = key_back[...], value_back[...]

    out, da = o_ref[...], da_ref[...].astype(jnp.float32)
    inverse = lax.rsqrt(jnp.mean(out * out, axis=-1, keepdims=True) + EPS)
    unit = out * inverse
    dgain_ref[...] += jnp.sum(da * unit, axis=0, keepdims=True)
    scaled = da * gain_ref[...]
    do = low(inverse * (scaled - unit * jnp.mean(scaled * unit, axis=-1, keepdims=True)))

    direct = product(q, k, NT)
    dmix = product(do, v, NT)
    dp_carried = from_start * product(do, low(value_start), NT)

    def intra_dp(factors):
        mask, late, early = factors
        return late * fine(jnp.where(mask, dmix, 0.0), early * fresh)

    def back_scores(dp):
        return weights * (dp - jnp.sum(weights * dp, axis=-1, keepdims=True))

    def intra_back(ds):
        def term(factors):
            mask, late, early = factors
            ds_late, p_late, factor = ds * late, weights * late, early * fresh
            return (
                jnp.where(mask, fine(ds_late, factor, NT), 0.0),
                jnp.where(mask, fine(p_late, factor, NT), 0.0),
                early
                * (
                    fine(jnp.where(mask, direct, 0.0), ds_late, TN)
                    + fine(jnp.where(mask, dmix, 0.0), p_late, TN)
                ),
            )

        return term

    def store(dp, parts):
        dp_ref[...] = dp
        da_part_ref[...], mix_ref[...], early_ref[...] = parts

    @pl.when(narrow)
    def _():
        factors = direct_factors(total)
        dp = intra_dp(factors) + dp_carried
        store(dp, intra_back(back_scores(dp) * scale)(factors))

    @pl.when(jnp.logical_not(narrow))
    def _():
        dp = over_levels(total, intra_dp, intra_dp) + dp_carried
        term = intra_back(back_scores(dp) * scale)
        store(dp, over_levels(total, term, term))

    dp = dp_ref[...]
    ds = back_scores(dp)
    ds_scaled = ds * scale
    ddirect, mix, early_sum = low(da_part_ref[...]), low(mix_ref[...]), early_ref[...]
    late_sum = ds * scores + weights * dp
    end_sum = to_end * (product(k, low(key_end), NT) + product(v, low(value_end), NT))
    carry = low(to_end * fresh)
    ds_start, p_start = low(ds_scaled * from_start), low(weights * from_start)

    dq = product(ddirect, k) + product(ds_start, low(key_start))
    dk = product(ddirect, q, TN) + product(carry, low(key_end))
    dv = product(mix, do, TN) + product(carry, low(value_end))
    draw_ref[:, :width] = low(dq * (q_sig * (1.0 + q_raw * (1.0 - q_sig))))
    draw_ref[:, width : 2 * width] = low(dk * (k_sig * (1.0 + k_raw * (1.0 - k_sig))))
    draw_ref[:, 2 * width : 3 * width] = low(dv)

    keep = jnp.exp(last)
    through = keep * row_of(
        jnp.sum(key_start * key_end + value_start * value_end, axis=1, keepdims=True)
    )
    after = (iota((size, size), 0) <= iota((size, size), 1)).astype(jnp.float32)
    before = (iota((size, size), 0) > iota((size, size), 1)).astype(jnp.float32)
    dlog = (
        fine(after, late_sum - fresh * early_sum)
        + fine(before, fresh * end_sum)
        + through
        - decay * (early_sum + end_sum)
    )
    dlogits = dlog * (1.0 / (1.0 + jnp.exp(logits))) / GATE_NORM
    dbias_ref[...] += jnp.sum(dlogits, axis=0, keepdims=True)
    dforget_ref[...] += fine(rank, dlogits, TN)
    draw_ref[:, 3 * width :] = low(fine(dlogits, forget, NT))

    keep_column = column_of(keep)
    key_back[...] = keep_column * key_end + product(ds_start, q, TN)
    value_back[...] = keep_column * value_end + product(p_start, do, TN)


def piece_specs(width, chunk, order):
    parts = [
        pl.BlockSpec((chunk, width), functools.partial(lambda part, i: (order(i), part), part))
        for part in range(3)
    ]
    rank = pl.BlockSpec((chunk, LANES), lambda i: (order(i), 3 * width // LANES))
    return parts + [rank]


def whole(shape):
    return pl.BlockSpec(shape, lambda i: (0,) * len(shape))


def mixer_forward(raw, forget, bias, gain):
    length, slots, width = raw.shape[0], bias.shape[1], gain.shape[1]
    steps = length // CHUNK

    def order(i):
        return i

    def rows(size):
        return pl.BlockSpec((CHUNK, size), lambda i: (order(i), 0))

    return pl.pallas_call(
        forward_kernel,
        grid=(steps,),
        in_specs=piece_specs(width, CHUNK, order)
        + [whole(forget.shape), whole(bias.shape), whole(gain.shape)],
        out_specs=(
            rows(width),
            rows(width),
            rows(2 * slots),
            pl.BlockSpec((1, 2, slots, width), lambda i: (i, 0, 0, 0)),
        ),
        out_shape=(
            jax.ShapeDtypeStruct((length, width), jnp.bfloat16),
            jax.ShapeDtypeStruct((length, width), jnp.float32),
            jax.ShapeDtypeStruct((length, 2 * slots), jnp.float32),
            jax.ShapeDtypeStruct((steps, 2, slots, width), jnp.float32),
        ),
        scratch_shapes=[
            pltpu.VMEM((slots, width), jnp.float32),
            pltpu.VMEM((slots, width), jnp.float32),
            pltpu.VMEM((CHUNK, slots), jnp.float32),
            pltpu.VMEM((CHUNK, CHUNK), jnp.float32),
        ],
        cost_estimate=pl.CostEstimate(
            flops=2 * length * width * 1024, bytes_accessed=length * width * 20, transcendentals=0
        ),
        name="mixer_forward",
    )(raw, raw, raw, raw, forget, bias, gain)


def mixer_backward(raw, out, soft, kept, da, forget, bias, gain):
    length, slots, width = raw.shape[0], bias.shape[1], gain.shape[1]
    steps = length // CHUNK

    def order(i):
        return steps - 1 - i

    def rows(size):
        return pl.BlockSpec((CHUNK, size), lambda i: (order(i), 0))

    return pl.pallas_call(
        backward_kernel,
        grid=(steps,),
        in_specs=piece_specs(width, CHUNK, order)
        + [
            rows(width),
            rows(2 * slots),
            pl.BlockSpec((1, 2, slots, width), lambda i: (order(i), 0, 0, 0)),
            rows(width),
            whole(forget.shape),
            whole(bias.shape),
            whole(gain.shape),
        ],
        out_specs=(
            rows(3 * width + LANES),
            whole(forget.shape),
            whole(bias.shape),
            whole(gain.shape),
        ),
        out_shape=(
            jax.ShapeDtypeStruct((length, 3 * width + LANES), jnp.bfloat16),
            jax.ShapeDtypeStruct(forget.shape, jnp.float32),
            jax.ShapeDtypeStruct(bias.shape, jnp.float32),
            jax.ShapeDtypeStruct(gain.shape, jnp.float32),
        ),
        scratch_shapes=[
            pltpu.VMEM((slots, width), jnp.float32),
            pltpu.VMEM((slots, width), jnp.float32),
            pltpu.VMEM((CHUNK, slots), jnp.float32),
            pltpu.VMEM((CHUNK, CHUNK), jnp.float32),
            pltpu.VMEM((CHUNK, CHUNK), jnp.float32),
            pltpu.VMEM((CHUNK, slots), jnp.float32),
        ],
        cost_estimate=pl.CostEstimate(
            flops=4 * length * width * 1024, bytes_accessed=length * width * 24, transcendentals=0
        ),
        name="mixer_backward",
    )(raw, raw, raw, raw, out, soft, kept, da, forget, bias, gain)


def inverse_rms(values):
    return lax.rsqrt(jnp.mean(values * values, axis=-1, keepdims=True) + EPS)


def norm_back(values, inverse, gain, grad):
    unit = values * inverse
    scaled = gain * grad
    grad_values = inverse * (scaled - unit * jnp.mean(scaled * unit, axis=-1, keepdims=True))
    return grad_values, jnp.sum(grad * unit, axis=0)


def shift(values, axis, step):
    count = lax.axis_size(axis)
    return lax.ppermute(values, axis, [(i, (i + step) % count) for i in range(count)])


def pass_on(values, axis, step):
    count = lax.axis_size(axis)
    pairs = [(i, i + step) for i in range(count) if 0 <= i + step < count]
    return lax.ppermute(values, axis, pairs)


def line_gather(values, axis, dim):
    count, place = lax.axis_size(axis), lax.axis_index(axis)
    size = values.shape[dim]
    shape = list(values.shape)
    shape[dim] = size * count
    up, down = [values], [values]
    for _ in range(count - 1):
        up.append(pass_on(up[-1], axis, 1))
        down.append(pass_on(down[-1], axis, -1))
    whole_array = lax.dynamic_update_slice_in_dim(
        jnp.zeros(shape, values.dtype), values, place * size, dim
    )
    for j in range(1, count):
        piece = jnp.where(place + j < count, down[j], up[count - j])
        whole_array = lax.dynamic_update_slice_in_dim(
            whole_array, piece, ((place + j) % count) * size, dim
        )
    return whole_array


def line_scatter(piece, axis):
    count, place = lax.axis_size(axis), lax.axis_index(axis)
    terms = {}

    def term(j):
        if j not in terms:
            terms[j] = piece(j)
        return terms[j]

    up = down = None
    for k in range(1, count):
        send_up = jnp.where(place < k, term(count - k), 0.0)
        send_down = jnp.where(place >= count - k, term(k), 0.0)
        if up is not None:
            send_up, send_down = send_up + up, send_down + down
        up = pass_on(low(send_up), axis, 1).astype(jnp.float32)
        down = pass_on(low(send_down), axis, -1).astype(jnp.float32)
    return term(0) + up + down


def exchange(piece, axis):
    count, place = lax.axis_size(axis), lax.axis_index(axis)
    own = piece(0)
    size = own.shape[0]
    received = lax.dynamic_update_slice_in_dim(
        jnp.zeros((size * count,) + own.shape[1:], own.dtype), own, place * size, 0
    )
    for j in range(1, count):
        received = lax.dynamic_update_slice_in_dim(
            received, shift(piece(j), axis, j), ((place - j) % count) * size, 0
        )
    return received


def total_sum(values, axes):
    for axis in axes:
        step = 1
        while step < lax.axis_size(axis):
            pairs = [(i, i ^ step) for i in range(lax.axis_size(axis))]
            values = values + lax.ppermute(values, axis, pairs)
            step *= 2
    return values


def local(
    tokens,
    valid,
    attn_gain,
    w_query,
    w_key,
    w_value,
    w_rank,
    w_forget,
    forget_bias,
    head_gain,
    w_out,
    mlp_gain,
    w_gate,
    w_up,
    w_down,
    cotangent,
):
    width = w_query.shape[0]
    head_size = width // HEADS
    slots = forget_bias.shape[0] // HEADS
    ranks = w_rank.shape[1]
    units = w_gate.shape[1]
    rows = tokens.shape[0]
    shards, shard = lax.axis_size("mp"), lax.axis_index("mp")
    copies = shards // HEADS
    own_width = width // shards
    head, part = shard // copies, shard % copies
    begin = shard * rows

    def rows_of(values, j):
        return lax.dynamic_slice_in_dim(values, ((shard + j) % shards) * rows, rows, 0)

    def head_columns(values, size):
        return lax.dynamic_slice_in_dim(values, head * size, size, values.ndim - 1)

    def own_part(values):
        if copies == 1:
            return values
        pieces = [
            lax.dynamic_slice_in_dim(values, i * head_size + part * own_width, own_width, 1)
            for i in range(values.shape[1] // head_size)
        ]
        return jnp.concatenate(pieces, axis=1)

    counted = (part == 0).astype(jnp.float32)
    own_mask = ((begin + jnp.arange(rows)) < valid[0])[:, None]
    own_cotangent = jnp.where(own_mask, cotangent, jnp.zeros_like(cotangent))
    gathered = line_gather(tokens, "mp", 0)
    grad_output = line_gather(own_cotangent, "mp", 0)

    w_inputs = jnp.concatenate(
        [head_columns(w, head_size) for w in (w_query, w_key, w_value)]
        + [jnp.pad(w_rank, ((0, 0), (0, LANES - ranks)))],
        axis=1,
    )
    w_hidden = jnp.concatenate([w_gate, w_up], axis=1)
    forget = jnp.pad(
        head_columns(w_forget.astype(jnp.float32), slots), ((0, LANES - ranks), (0, 0))
    )
    bias = head_columns(forget_bias, slots)[None]
    gain = head_gain[None]

    resid = gathered.astype(jnp.float32)
    unit_input = resid * inverse_rms(resid)
    normed = low(unit_input * attn_gain)
    raw = product(normed, w_inputs)
    a_head, mixed, soft, kept = mixer_forward(raw, forget, bias, gain)
    a_all = line_gather(own_part(a_head), "mp", 1)
    hidden = resid + product(a_all, w_out)
    unit_hidden = hidden * inverse_rms(hidden)
    mlp_normed = low(unit_hidden * mlp_gain)
    both = product(mlp_normed, w_hidden)
    gate, up = both[:, :units], both[:, units:]
    activated = jax.nn.silu(gate)
    inner = low(activated * up)

    def dp_sum(values, axis):
        return lax.psum_scatter(
            low(values), "dp", scatter_dimension=axis, tiled=True
        ).astype(jnp.float32)

    sum_down = dp_sum(product(inner, grad_output, TN), 1)
    grad_inner = product(grad_output, w_down, NT)
    grad_both = jnp.concatenate(
        [low(grad_inner * up * silu_slope(gate)), low(grad_inner * activated)], axis=1
    )
    partial = {}

    def grad_normed_piece(j):
        partial[j] = product(rows_of(grad_both, j), w_hidden, NT)
        return partial[j]

    grad_normed = line_scatter(grad_normed_piece, "mp")
    part_mlp_gain = sum(
        jnp.sum(values * rows_of(unit_hidden, j), axis=0) for j, values in partial.items()
    )
    sum_both = dp_sum(product(mlp_normed, grad_both, TN), 0)

    own_hidden = rows_of(hidden, 0)
    grad_hidden, _ = norm_back(own_hidden, inverse_rms(own_hidden), mlp_gain, grad_normed)
    grad_hidden = grad_hidden + own_cotangent.astype(jnp.float32)
    grad_hidden_low = low(grad_hidden)
    grad_a_own = low(product(grad_hidden_low, w_out, NT))

    def head_of(j):
        return lax.dynamic_slice_in_dim(
            grad_a_own, (((shard + j) % shards) // copies) * head_size, head_size, 1
        )

    def columns_of(j):
        return lax.dynamic_slice_in_dim(
            grad_hidden_low, ((shard + j) % shards) * own_width, own_width, 1
        )

    grad_a = exchange(head_of, "mp")
    draw, part_forget, part_bias, part_head_gain = mixer_backward(
        raw, mixed, soft, kept, grad_a, forget, bias, gain
    )
    draw_inputs = own_part(draw[:, : 3 * head_size])
    draw_rank = draw[:, 3 * head_size :]
    if copies > 1:
        draw_rank = low(draw_rank.astype(jnp.float32) * counted)
        w_own = jnp.concatenate(
            [own_part(w_inputs[:, : 3 * head_size]), w_inputs[:, 3 * head_size :]], axis=1
        )
        draw = jnp.concatenate([draw_inputs, draw_rank], axis=1)
    else:
        w_own = w_inputs
    partial_input = {}

    def grad_input_piece(j):
        partial_input[j] = product(rows_of(draw, j), w_own, NT)
        return partial_input[j]

    grad_input = line_scatter(grad_input_piece, "mp")
    part_attn_gain = sum(
        jnp.sum(values * rows_of(unit_input, j), axis=0) for j, values in partial_input.items()
    )
    own_resid = tokens.astype(jnp.float32)
    grad_resid, _ = norm_back(own_resid, inverse_rms(own_resid), attn_gain, grad_input)
    grad_tokens = grad_hidden + grad_resid

    mlp_own = line_scatter(lambda j: product(rows_of(inner, j), w_down), "mp")
    output = low(jnp.where(own_mask, own_hidden + mlp_own, 0.0))

    own_grad_hidden = exchange(columns_of, "mp")
    sum_inputs = dp_sum(
        jnp.concatenate(
            [
                low(product(normed, draw_inputs, TN)),
                low(product(a_all, own_grad_hidden, TN)),
            ],
            axis=1,
        ),
        0,
    )
    sum_query, sum_key, sum_value, sum_wout = (
        sum_inputs[:, i * own_width : (i + 1) * own_width] for i in range(4)
    )
    part_rank = product(draw_rank[:, :ranks], normed, TN)

    def placed(values):
        spread = jnp.zeros((values.shape[0], HEADS * slots), jnp.float32)
        return lax.dynamic_update_slice_in_dim(spread, values * counted, head * slots, 1)

    def lines(values):
        flat = values.reshape(-1)
        return jnp.pad(flat, (0, -flat.shape[0] % width)).reshape(-1, width)

    small = [
        part_rank,
        part_attn_gain,
        part_mlp_gain,
        placed(part_forget[:ranks]),
        placed(part_bias),
        part_head_gain * counted,
    ]
    packed = total_sum(jnp.concatenate([lines(values) for values in small]), ("mp", "dp"))
    replicas, replica = lax.axis_size("dp"), lax.axis_index("dp")
    own_small = []
    line = 0
    for values in small:
        size, last = values.size, values.shape[-1]
        count = -(-size // width)
        summed = packed[line : line + count].reshape(-1)[:size].reshape(-1, last)
        line += count
        own_small.append(
            lax.dynamic_slice_in_dim(summed, replica * (last // replicas), last // replicas, 1)
        )
    sum_rank, sum_attn_gain, sum_mlp_gain, sum_forget, sum_bias, sum_head_gain = own_small
    return (
        output,
        grad_tokens,
        sum_attn_gain[0],
        sum_query,
        sum_key,
        sum_value,
        sum_rank.T,
        sum_forget,
        sum_bias[0],
        sum_head_gain[0],
        sum_wout,
        sum_mlp_gain[0],
        sum_both[:, :units],
        sum_both[:, units:],
        sum_down,
    )


def solution(mesh):
    return jax.shard_map(
        local,
        mesh=mesh,
        in_specs=(
            P(("dp", "mp"), None),
            P("dp"),
            P(),
            P(),
            P(),
            P(),
            P(),
            P(),
            P(),
            P(),
            P(),
            P(),
            P(None, "mp"),
            P(None, "mp"),
            P("mp", None),
            P(("dp", "mp"), None),
        ),
        out_specs=(
            P(("dp", "mp"), None),
            P(("dp", "mp"), None),
            P("dp"),
            P("dp", "mp"),
            P("dp", "mp"),
            P("dp", "mp"),
            P("dp", None),
            P(None, "dp"),
            P("dp"),
            P("dp"),
            P("dp", "mp"),
            P("dp"),
            P("dp", "mp"),
            P("dp", "mp"),
            P("mp", "dp"),
        ),
        check_vma=False,
    )
```
